32 devices in a mesh: pts: 4 (over y, core), ctr: 8 (over z, x).
Axes of the slice: x: 2, y: 2, z: 4, core: 2. Of those that a mesh axis runs over, the one named last changes fastest.
Arguments:
- points: bfloat16 [512, 512], P(('pts', 'ctr')), may hold values from -6 to 6
- point_class: int32 [512], P(('pts', 'ctr')), may hold values from 0 to 7
- targets: float32 [512, 128], P(('pts', 'ctr')), may hold values from -6 to 6
- class_weight: float32 [8], replicated, may hold values from 0.25 to 4
- inv_scale: float32 [512], replicated, may hold values from 0.003 to 0.3
- centers: bfloat16 [32768, 512], P('ctr'), may hold values from -6 to 6
- coefficients: bfloat16 [32768, 128], P('ctr'), may hold values from -2.5 to 2.5
- center_index: int32 [4096], replicated, may hold values from 0 to 32767, as said below
- factor: float32 [4096, 4096], P('ctr'), as said below
- panel_inverse: float32 [4096, 2048], P('ctr'), as said below
Outputs:
- gradient: float32 [32768, 128], P('ctr', 'pts')
- solved: float32 [4096, 128], P('ctr', 'pts')
The draws below stay inside these ranges and needn't reach their ends.
Inputs may be any that keep to these rules, and one draw needn't show every extreme that they name: `center_index`: the values are distinct; window row r lies in the center shard (index of ctr, 4096 centers each) numbered order[r mod 8] for one permutation order of the shards, so each shard holds exactly 512 window rows and the 512 rows of each aligned block of the window hold at most 64 of one shard's centers, a bound that is reached. factor is lower triangular with its diagonal between 1 and 2. `panel_inverse`: the rows of panel p hold the inverse of factor's diagonal block of rows and columns p * 2048 to (p + 1) * 2048 - 1.
All inputs are finite; a program needn't handle non-finite values.
Results may differ from the reference program's by a relative error of at most 0.0055.
Values may be sent and summed in bfloat16 or wider, within the bound.
A program may use at most 64 MiB of HBM per device.

```python
import math
import jax
import jax.numpy as jnp
from jax import lax

D = 512
TARGETS = 128
CLASSES = 8
CTR_DEV = 4096
PANEL = 2048
PANELS = 2
NPTS = 512
CENTERS = 32768
WIN = 4096
N_CTR = 8


def factor_matrix(key):
    folded = jax.random.fold_in(key, 11)
    strict_key, diagonal_key = jax.random.split(folded)
    strict = jnp.tril(jax.random.normal(strict_key, (WIN, WIN), jnp.float32), -1) * (0.6 / math.sqrt(WIN))
    diagonal = jax.random.uniform(diagonal_key, (WIN,), jnp.float32, 1.0, 2.0)
    return strict + jnp.diag(diagonal)


def draw_factor(key, part):
    return factor_matrix(key)


def draw_panel_inverse(key, part):
    matrix = factor_matrix(key)
    identity = jnp.eye(PANEL, dtype=jnp.float32)
    blocks = []
    for current in range(PANELS):
        begin = current * PANEL
        diagonal_block = matrix[begin:begin + PANEL, begin:begin + PANEL]
        blocks.append(jax.scipy.linalg.solve_triangular(diagonal_block, identity, lower=True))
    return jnp.concatenate(blocks, axis=0)


def draw_center_index(key, part):
    folded = jax.random.fold_in(key, 5)
    order_key, offset_key = jax.random.split(folded)
    shard_order = jax.random.permutation(order_key, N_CTR).astype(jnp.int32)
    rows = jnp.arange(WIN, dtype=jnp.int32)
    shard = shard_order[rows % N_CTR]
    occurrence = rows // N_CTR
    offset_keys = jax.random.split(offset_key, N_CTR)
    offsets = jax.vmap(lambda single: jax.random.permutation(single, CTR_DEV).astype(jnp.int32))(offset_keys)
    return (shard * CTR_DEV + offsets[shard, occurrence]).astype(jnp.int32)


def set_ends(drawn, key, least, top_value):
    spot = [jax.random.randint(jax.random.fold_in(key, axis), (), 0, length) for axis, length in enumerate(drawn.shape)]
    main_axis = drawn.shape.index(max(drawn.shape))
    beside = spot[:main_axis] + [(spot[main_axis] + 1) % drawn.shape[main_axis]] + spot[main_axis + 1:]
    return drawn.at[tuple(spot)].set(least).at[tuple(beside)].set(top_value)


def shard_levels(rng, dims, pieces, smallest, top_value):
    level = 1.0
    for position, parts in pieces:
        draws = jax.random.uniform(jax.random.fold_in(jax.random.fold_in(rng, 6), position), (parts,), jnp.float32, smallest / len(pieces), top_value / len(pieces))
        level = level * jnp.repeat(jnp.exp(draws), dims[position] // parts).reshape((-1,) + (1,) * (len(dims) - 1 - position))
    return level


def noise(key, shape, scale, most, pieces=(), held_as=jnp.bfloat16):
    gain = shard_levels(key, shape, pieces, -0.22, 0.18) if pieces else 1.0
    entries = jax.random.normal(key, shape, jnp.float32) * scale * gain
    return jnp.minimum(jnp.maximum(entries, -most), most).astype(held_as)


def setup_inputs(seed: int = 0) -> dict:
    streams_of = jax.random.split(jax.random.key(seed), 11)
    points = noise(streams_of[0], (NPTS, D), 1.0, 6.0, ((0, 32),))
    point_class = set_ends(jax.random.randint(streams_of[1], (NPTS,), 0, CLASSES), jax.random.fold_in(streams_of[1], 1), 0, CLASSES - 1).astype(jnp.int32)
    targets = noise(streams_of[2], (NPTS, TARGETS), 1.0, 6.0, ((0, 32),), jnp.float32)
    class_weight = jnp.clip(jnp.exp(jax.random.uniform(streams_of[3], (CLASSES,), jnp.float32, math.log(0.25), math.log(4.0))), 0.25, 4.0)
    inv_scale = jnp.clip(jnp.exp(jax.random.uniform(streams_of[4], (D,), jnp.float32, math.log(0.003), math.log(0.3))), 0.003, 0.3)
    centers = noise(streams_of[5], (CENTERS, D), 1.0, 6.0, ((0, 8),))
    coefficients = noise(streams_of[6], (CENTERS, TARGETS), 0.35, 2.5, ((0, 8),))
    center_index = draw_center_index(jax.random.fold_in(streams_of[10], 71), 0)
    factor = draw_factor(jax.random.fold_in(streams_of[10], 71), 0)
    panel_inverse = draw_panel_inverse(jax.random.fold_in(streams_of[10], 71), 0)
    return dict(points=points, point_class=point_class, targets=targets, class_weight=class_weight, inv_scale=inv_scale, centers=centers, coefficients=coefficients, center_index=center_index, factor=factor, panel_inverse=panel_inverse)


def gaussian(samples, anchors):
    products = lax.dot_general(samples.astype(jnp.float32), anchors.astype(jnp.float32), (((1,), (1,)), ((), ())), preferred_element_type=jnp.float32)
    left_norm = jnp.sum(jnp.square(samples.astype(jnp.float32)), axis=1)
    right_norm = jnp.sum(jnp.square(anchors.astype(jnp.float32)), axis=1)
    exponent = products - 0.5 * left_norm[:, None] - 0.5 * right_norm[None, :]
    return jnp.exp(exponent).astype(jnp.bfloat16)

def class_lookup(labels, table):
    classes = jnp.arange(table.shape[0], dtype=jnp.int32)
    return jnp.sum(jnp.where(labels[:, None] == classes[None, :], table[None, :], 0.0), axis=1)

def reference(points, point_class, targets, class_weight, inv_scale, centers, coefficients, center_index, factor, panel_inverse):
    scaled_points = (points.astype(jnp.float32) * inv_scale[None, :]).astype(jnp.bfloat16)
    scaled_centers = (centers.astype(jnp.float32) * inv_scale[None, :]).astype(jnp.bfloat16)
    center_blocks = scaled_centers.reshape(N_CTR, CTR_DEV, D)
    coef_blocks = coefficients.reshape(N_CTR, CTR_DEV, TARGETS)

    def accumulate(running, inputs):
        center_block, coef_block = inputs
        kernel = gaussian(scaled_points, center_block)
        return (running + jnp.dot(kernel.astype(jnp.float32), coef_block.astype(jnp.float32), preferred_element_type=jnp.float32), None)
    predicted, unused = lax.scan(accumulate, jnp.zeros((NPTS, TARGETS), jnp.float32), (center_blocks, coef_blocks))
    weight = class_lookup(point_class, class_weight)
    residual = (weight[:, None] * (predicted - targets)).astype(jnp.bfloat16)

    def backward(center_block):
        kernel = gaussian(scaled_points, center_block)
        return lax.dot_general(kernel.astype(jnp.float32), residual.astype(jnp.float32), (((0,), (0,)), ((), ())), preferred_element_type=jnp.float32)
    gradient = lax.map(backward, center_blocks).reshape(CENTERS, TARGETS)
    window = gradient[center_index]
    solved_full = jnp.zeros((WIN, TARGETS), jnp.float32)
    for current in range(PANELS):
        begin = current * PANEL
        rhs_part = window[begin:begin + PANEL]
        if current > 0:
            rhs_part = rhs_part - jnp.dot(factor[begin:begin + PANEL], solved_full, precision=lax.Precision.HIGHEST)
        panel_part = jnp.dot(panel_inverse[begin:begin + PANEL], rhs_part, precision=lax.Precision.HIGHEST)
        solved_full = solved_full.at[begin:begin + PANEL].set(panel_part)
    return (gradient, solved_full)
```

```python
import functools

import jax
import jax.numpy as jnp
from jax import lax
from jax.experimental import pallas as pl
from jax.experimental.pallas import tpu as pltpu
from jax.sharding import PartitionSpec as P

MESH = pl.DeviceIdType.MESH
NT = (((1,), (1,)), ((), ()))
F32 = jnp.float32
BF16 = jnp.bfloat16


def dot_nt(left, right):
    return lax.dot_general(left, right, NT, preferred_element_type=F32)


def kernel(
    n_pts, n_ctr, panels, chunk,
    order_ref, pts_ref, cls_ref, tgt_ref, cw_ref, inv_ref, sel_ref, cen_hbm, coef_hbm, fac_hbm, pinv_hbm,
    grad_ref, sol_ref,
    cen, coef, pinv_raw, pinv, fac_raw, fac, rnorm, pall, kmat, ksel,
    part, part_recv, rall, wsend, wrecv, wpack, wblk, solsend, solrecv, rhssend, rhsrecv,
    loc, pt_s, pt_r, fw_s, fw_r, pr_s, pr_r, rs_s, rs_r, w_s, w_r, so_s, so_r, rh_s, rh_r,
):
    p_me, c_me = lax.axis_index("pts"), lax.axis_index("ctr")
    rows = pts_ref.shape[0]
    group = rows * n_ctr
    centers = cen.shape[0]
    feats = cen.shape[1]
    targets = tgt_ref.shape[1]
    tcols = targets // n_pts
    own_rows = pinv.shape[0]
    panel_rows = pinv.shape[1]
    owners = panel_rows // own_rows
    my_panel = c_me // owners
    chunks = centers // chunk

    def remote(src, dst, send, recv, p, c):
        return pltpu.make_async_remote_copy(
            src_ref=src, dst_ref=dst, send_sem=send, recv_sem=recv,
            device_id={"pts": p, "ctr": c}, device_id_type=MESH,
        )

    def each(n, fn):
        def step(k, carry):
            fn(k)
            return carry
        lax.fori_loop(0, n, step, 0)

    barrier = pltpu.get_barrier_semaphore()
    everyone = n_pts * n_ctr
    me = p_me * n_ctr + c_me

    def greet(k):
        other = lax.rem(me + k + 1, everyone)
        pl.semaphore_signal(
            barrier, inc=1,
            device_id={"pts": other // n_ctr, "ctr": lax.rem(other, n_ctr)}, device_id_type=MESH,
        )
    each(everyone - 1, greet)

    cen_copy = pltpu.make_async_copy(cen_hbm, cen, loc.at[0])
    coef_copy = pltpu.make_async_copy(coef_hbm, coef, loc.at[1])
    pinv_copy = pltpu.make_async_copy(pinv_hbm, pinv_raw, loc.at[2])
    fac_copy = pltpu.make_async_copy(fac_hbm.at[:, pl.ds(0, fac.shape[1])], fac_raw, loc.at[3])
    for copy in (cen_copy, coef_copy, pinv_copy, fac_copy):
        copy.start()

    inv = inv_ref[...]
    own_slot = pl.ds(pl.multiple_of(me * rows, rows), rows)
    pall[own_slot, :] = (pts_ref[...].astype(F32) * inv).astype(BF16)
    pl.semaphore_wait(barrier, everyone - 1)

    def pt_copy(c_src, c_dst):
        slot = pl.ds(pl.multiple_of((p_me * n_ctr + c_src) * rows, rows), rows)
        return remote(pall.at[slot], pall.at[slot], pt_s.at[c_dst], pt_r.at[c_src], p_me, c_dst)

    def peer(k):
        return lax.rem(c_me + k + 1, n_ctr)
    each(n_ctr - 1, lambda k: pt_copy(c_me, peer(k)).start())

    ones = jnp.ones((8, feats), BF16)
    cen_copy.wait()

    def scale(k):
        at = pl.ds(pl.multiple_of(k * chunk, chunk), chunk)
        scaled = (cen[at, :].astype(F32) * inv).astype(BF16)
        cen[at, :] = scaled
        square = jnp.square(scaled.astype(F32))
        high = square.astype(BF16)
        low = (square - high.astype(F32)).astype(BF16)
        rnorm[:, at] = 0.5 * (dot_nt(ones, high) + dot_nt(ones, low))
    each(chunks, scale)
    coef_copy.wait()

    each(n_ctr - 1, lambda k: pt_copy(peer(k), peer(k)).wait_recv())

    def group_at(p):
        return pl.ds(pl.multiple_of(p * group, group), group)

    def fw_copy(p_src, p_dst):
        at = group_at(p_src)
        return remote(pall.at[at], pall.at[at], fw_s.at[p_dst], fw_r.at[p_src], p_dst, c_me)

    def mate(k):
        return lax.rem(p_me + k + 1, n_pts)
    each(n_pts - 1, lambda k: fw_copy(p_me, mate(k)).start())

    def half_norm(x):
        return 0.5 * jnp.sum(jnp.square(x.astype(F32)), axis=1, keepdims=True)

    def kernel_block(p, k):
        at = pl.ds(pl.multiple_of(k * chunk, chunk), chunk)
        mine = pall[group_at(p), :]
        exponent = dot_nt(mine, cen[at, :]) - half_norm(mine) - rnorm[0:1, at]
        block = jnp.exp(exponent).astype(BF16)
        kmat[group_at(p), at] = block
        return block, at

    def forward(k, total):
        block, at = kernel_block(p_me, k)
        return total + jnp.dot(block, coef[at, :], preferred_element_type=F32)
    total = lax.fori_loop(0, chunks, forward, jnp.zeros((group, targets), F32))
    part[...] = total.reshape(n_ctr, rows, targets)

    def pr_copy(c_src, c_dst):
        return remote(part.at[c_dst], part_recv.at[c_src], pr_s.at[c_dst], pr_r.at[c_src], p_me, c_dst)
    each(n_ctr - 1, lambda k: pr_copy(c_me, peer(k)).start())

    pinv_copy.wait()
    pinv[...] = pinv_raw[...].astype(BF16)
    fac_copy.wait()
    fac[...] = fac_raw[...].astype(BF16)

    each(n_ctr - 1, lambda k: pr_copy(peer(k), peer(k)).wait_recv())
    part_recv[c_me] = part[c_me]
    predicted = jnp.sum(part_recv[...], axis=0)
    classes = lax.broadcasted_iota(jnp.int32, (rows, cw_ref.shape[1]), 1)
    weight = jnp.sum(jnp.where(cls_ref[...] == classes, cw_ref[...], 0.0), axis=1, keepdims=True)
    rall[own_slot, :] = (weight * (predicted - tgt_ref[...])).astype(BF16)

    def rs_copy(src, dst):
        slot = pl.ds(pl.multiple_of(src * rows, rows), rows)
        return remote(
            rall.at[slot], rall.at[slot], rs_s.at[dst], rs_r.at[src], dst // n_ctr, lax.rem(dst, n_ctr)
        )

    def other(k):
        return lax.rem(me + k + 1, everyone)
    each(everyone - 1, lambda k: rs_copy(me, other(k)).start())

    each(n_pts - 1, lambda k: fw_copy(mate(k), mate(k)).wait_recv())

    def rest(k):
        kernel_block(mate(k // chunks), lax.rem(k, chunks))
    each((n_pts - 1) * chunks, rest)

    chosen = (sel_ref[...].astype(F32) * inv).astype(BF16)
    chosen_norm = half_norm(chosen)

    def window_kernel(p):
        mine = pall[group_at(p), :]
        square = jnp.square(mine.astype(F32))
        high = square.astype(BF16)
        low = (square - high.astype(F32)).astype(BF16)
        norm = 0.5 * (dot_nt(ones, high) + dot_nt(ones, low))
        ksel[:, group_at(p)] = jnp.exp(dot_nt(chosen, mine) - norm[0:1] - chosen_norm).astype(BF16)
    each(n_pts, window_kernel)

    each(everyone - 1, lambda k: rs_copy(other(k), other(k)).wait_recv())

    source = lax.broadcasted_iota(jnp.int32, (targets, targets), 0)
    lane = lax.broadcasted_iota(jnp.int32, (targets, targets), 1)
    pick = (source == p_me * tcols + lax.rem(lane, tcols)).astype(BF16)
    wide = jnp.dot(rall[...], pick, preferred_element_type=F32).astype(BF16)
    window = jnp.dot(ksel[...], wide, preferred_element_type=F32)
    run = wsend.shape[1]
    lane_group = lax.broadcasted_iota(jnp.int32, (run, targets), 1) // tcols
    for panel in range(panels):
        packed = jnp.zeros((run, targets), F32)
        for g in range(n_pts):
            begin = (panel * n_pts + g) * run
            packed = packed + jnp.where(lane_group == g, window[begin:begin + run], 0.0)
        wsend[panel] = packed.astype(BF16)

    def w_copy(c_src, c_dst):
        return remote(
            wsend.at[c_dst // owners], wrecv.at[c_src], w_s.at[c_dst], w_r.at[c_src], p_me, c_dst
        )
    each(n_ctr - 1, lambda k: w_copy(c_me, peer(k)).start())
    wrecv[c_me] = wsend[my_panel]

    tall = lax.broadcasted_iota(jnp.int32, (tcols, targets), 1)
    first = lax.broadcasted_iota(jnp.int32, (tcols, targets), 0)
    pick_t = (tall == p_me * tcols + first).astype(BF16)
    wide_t = dot_nt(pick_t, rall[...]).astype(BF16)

    def backward(k):
        at = pl.ds(pl.multiple_of(k * chunk, chunk), chunk)
        grad_ref[:, at] = jnp.dot(wide_t, kmat[:, at], preferred_element_type=F32)
    each(chunks, backward)

    each(n_ctr - 1, lambda k: w_copy(peer(k), peer(k)).wait_recv())
    for o in range(n_ctr):
        wpack[pl.ds(o, run, stride=n_ctr), :] = wrecv[order_ref[o]].astype(F32)

    def so_copy(c_src, c_dst):
        return remote(solsend, solrecv.at[c_src], so_s.at[c_dst], so_r.at[c_src], p_me, c_dst)

    def rh_copy(c_src, c_dst):
        at = lax.rem(c_src, owners)
        return remote(rhssend, rhsrecv.at[at], rh_s.at[c_dst], rh_r.at[at], p_me, c_dst)

    for panel in range(panels):
        @pl.when(my_panel == panel)
        def _():
            if panel == 0:
                turned = wpack[...].T.astype(BF16)
                rhs = jnp.concatenate([turned[g * tcols:(g + 1) * tcols] for g in range(n_pts)], axis=1)
            else:
                local = (c_me - panel * owners) * own_rows
                part_len = panel_rows // n_pts
                within = pl.multiple_of(lax.rem(local, part_len), own_rows)
                turned = wpack[pl.ds(within, own_rows), :].T
                for g in range(n_pts):
                    wblk[g] = turned[g * tcols:(g + 1) * tcols]
                own = wblk[local // part_len]
                done = panel * owners
                each(done, lambda k: so_copy(k, k).wait_recv())
                solved = jnp.concatenate([solrecv[b] for b in range(done)], axis=1)
                own = own - dot_nt(solved, fac[:, :done * own_rows])
                rhssend[...] = own.astype(BF16)

                def fellow(k):
                    return panel * owners + lax.rem(c_me - panel * owners + k + 1, owners)
                each(owners - 1, lambda k: rh_copy(c_me, fellow(k)).start())
                rhsrecv[c_me - panel * owners] = rhssend[...]
                each(owners - 1, lambda k: rh_copy(fellow(k), fellow(k)).wait_recv())
                rhs = jnp.concatenate([rhsrecv[b] for b in range(owners)], axis=1)
            result = dot_nt(rhs, pinv[...])
            sol_ref[...] = result
            later = (panels - 1 - panel) * owners
            if later:
                solsend[...] = result.astype(BF16)

                def after(k):
                    return (panel + 1) * owners + lax.rem(k + c_me, later)
                each(later, lambda k: so_copy(c_me, after(k)).start())
                each(later, lambda k: so_copy(c_me, after(k)).wait_send())
            if panel > 0:
                each(owners - 1, lambda k: rh_copy(c_me, fellow(k)).wait_send())

    each(n_ctr - 1, lambda k: pt_copy(c_me, peer(k)).wait_send())
    each(n_pts - 1, lambda k: fw_copy(p_me, mate(k)).wait_send())
    each(n_ctr - 1, lambda k: pr_copy(c_me, peer(k)).wait_send())
    each(everyone - 1, lambda k: rs_copy(me, other(k)).wait_send())
    each(n_ctr - 1, lambda k: w_copy(c_me, peer(k)).wait_send())


def body(
    points, point_class, targets, class_weight, inv_scale, centers, coefficients, center_index, factor, panel_inverse
):
    n_pts, n_ctr = lax.axis_size("pts"), lax.axis_size("ctr")
    rows, feats = points.shape
    n_cen, n_tgt = coefficients.shape
    tcols = n_tgt // n_pts
    own_rows, panel_rows = panel_inverse.shape
    panels = factor.shape[1] // panel_rows
    owners = panel_rows // own_rows
    everyone = n_pts * n_ctr
    total = rows * everyone
    slots = center_index.shape[0] // n_ctr
    run = slots // panels // n_pts
    solved_cols = panel_rows * (panels - 1)
    mine = lax.axis_index("ctr")
    order = center_index[:n_ctr] // n_cen
    table = center_index.reshape(slots, n_ctr)
    local = jnp.sum(jnp.where((order == mine)[None, :], table - mine * n_cen, 0), axis=1)
    chosen = centers.at[local].get(mode="promise_in_bounds")
    vmem = pl.BlockSpec(memory_space=pltpu.VMEM)
    hbm = pl.BlockSpec(memory_space=pl.ANY)
    dma = pltpu.SemaphoreType.DMA
    grad, solved = pl.pallas_call(
        functools.partial(kernel, n_pts, n_ctr, panels, 512),
        out_shape=(
            jax.ShapeDtypeStruct((tcols, n_cen), F32),
            jax.ShapeDtypeStruct((tcols, own_rows), F32),
        ),
        in_specs=[pl.BlockSpec(memory_space=pltpu.SMEM)] + [vmem] * 6 + [hbm] * 4,
        out_specs=(vmem, vmem),
        scratch_shapes=[
            pltpu.VMEM((n_cen, feats), BF16),
            pltpu.VMEM((n_cen, n_tgt), BF16),
            pltpu.VMEM((own_rows, panel_rows), F32),
            pltpu.VMEM((own_rows, panel_rows), BF16),
            pltpu.VMEM((own_rows, solved_cols), F32),
            pltpu.VMEM((own_rows, solved_cols), BF16),
            pltpu.VMEM((8, n_cen), F32),
            pltpu.VMEM((total, feats), BF16),
            pltpu.VMEM((total, n_cen), BF16),
            pltpu.VMEM((slots, total), BF16),
            pltpu.VMEM((n_ctr, rows, n_tgt), F32),
            pltpu.VMEM((n_ctr, rows, n_tgt), F32),
            pltpu.VMEM((total, n_tgt), BF16),
            pltpu.VMEM((panels, run, n_tgt), BF16),
            pltpu.VMEM((n_ctr, run, n_tgt), BF16),
            pltpu.VMEM((run * n_ctr, n_tgt), F32),
            pltpu.VMEM((n_pts, tcols, own_rows), F32),
            pltpu.VMEM((tcols, own_rows), BF16),
            pltpu.VMEM((owners * (panels - 1), tcols, own_rows), BF16),
            pltpu.VMEM((tcols, own_rows), BF16),
            pltpu.VMEM((owners, tcols, own_rows), BF16),
            dma((4,)),
            dma((n_ctr,)), dma((n_ctr,)),
            dma((n_pts,)), dma((n_pts,)),
            dma((n_ctr,)), dma((n_ctr,)),
            dma((everyone,)), dma((everyone,)),
            dma((n_ctr,)), dma((n_ctr,)),
            dma((n_ctr,)), dma((n_ctr,)),
            dma((n_ctr,)), dma((owners,)),
        ],
        compiler_params=pltpu.CompilerParams(
            collective_id=0, has_side_effects=True, vmem_limit_bytes=67043328
        ),
        name="falkon",
    )(
        order, points, point_class[:, None], targets, class_weight[None, :], inv_scale[None, :],
        chosen, centers, coefficients, factor, panel_inverse,
    )
    return grad.T, solved.T


def solution(mesh):
    placed = (
        P(("pts", "ctr"), None),
        P(("pts", "ctr")),
        P(("pts", "ctr"), None),
        P(),
        P(),
        P("ctr", None),
        P("ctr", None),
        P(),
        P("ctr", None),
        P("ctr", None),
    )
    return jax.shard_map(
        body,
        mesh=mesh,
        in_specs=placed,
        out_specs=(P("ctr", "pts"), P("ctr", "pts")),
        check_vma=False,
    )
```

```python
import functools

import jax
import jax.numpy as jnp
from jax import lax
from jax.experimental import pallas as pl
from jax.experimental.pallas import tpu as pltpu
from jax.sharding import PartitionSpec as P

MESH = pl.DeviceIdType.MESH
NT = (((1,), (1,)), ((), ()))
F32 = jnp.float32
BF16 = jnp.bfloat16


def dot_nt(left, right):
    return lax.dot_general(left, right, NT, preferred_element_type=F32)


def kernel(
    n_pts, n_ctr, panels, chunk,
    pts_ref, cls_ref, tgt_ref, cw_ref, inv_ref, idx_ref, idx_hbm, cen_hbm, coef_hbm, fac_hbm, pinv_hbm,
    grad_ref, sol_ref,
    cen, coef, pinv_raw, pinv, fac_raw, fac, rnorm, pall, kmat, ksel,
    head, sel, part, part_recv, rall, wsend, wrecv, wpack, wblk, solsend, solrecv, rhssend, rhsrecv,
    loc, pt_s, pt_r, fw_s, fw_r, pr_s, pr_r, rs_s, rs_r, w_s, w_r, so_s, so_r, rh_s, rh_r,
):
    p_me, c_me = lax.axis_index("pts"), lax.axis_index("ctr")
    rows = pts_ref.shape[0]
    group = rows * n_ctr
    centers = cen.shape[0]
    feats = cen.shape[1]
    targets = tgt_ref.shape[1]
    tcols = targets // n_pts
    own_rows = pinv.shape[0]
    panel_rows = pinv.shape[1]
    owners = panel_rows // own_rows
    my_panel = c_me // owners
    chunks = centers // chunk

    def remote(src, dst, send, recv, p, c):
        return pltpu.make_async_remote_copy(
            src_ref=src, dst_ref=dst, send_sem=send, recv_sem=recv,
            device_id={"pts": p, "ctr": c}, device_id_type=MESH,
        )

    def each(n, fn):
        def step(k, carry):
            fn(k)
            return carry
        lax.fori_loop(0, n, step, 0)

    barrier = pltpu.get_barrier_semaphore()
    everyone = n_pts * n_ctr
    me = p_me * n_ctr + c_me

    def greet(k):
        other = lax.rem(me + k + 1, everyone)
        pl.semaphore_signal(
            barrier, inc=1,
            device_id={"pts": other // n_ctr, "ctr": lax.rem(other, n_ctr)}, device_id_type=MESH,
        )
    cen_copy = pltpu.make_async_copy(cen_hbm, cen, loc.at[0])
    coef_copy = pltpu.make_async_copy(coef_hbm, coef, loc.at[1])
    pinv_copy = pltpu.make_async_copy(pinv_hbm, pinv_raw, loc.at[2])
    fac_copy = pltpu.make_async_copy(fac_hbm.at[:, pl.ds(0, fac.shape[1])], fac_raw, loc.at[3])
    head_copy = pltpu.make_async_copy(idx_hbm.at[pl.ds(0, head.shape[0])], head, loc.at[4])
    cen_copy.start()
    each(everyone - 1, greet)
    coef_copy.start()

    inv = inv_ref[...]
    own_slot = pl.ds(pl.multiple_of(me * rows, rows), rows)
    pall[own_slot, :] = (pts_ref[...].astype(F32) * inv).astype(BF16)
    pl.semaphore_wait(barrier, everyone - 1)

    def pt_copy(c_src, c_dst):
        slot = pl.ds(pl.multiple_of((p_me * n_ctr + c_src) * rows, rows), rows)
        return remote(pall.at[slot], pall.at[slot], pt_s.at[c_dst], pt_r.at[c_src], p_me, c_dst)

    def peer(k):
        return lax.rem(c_me + k + 1, n_ctr)
    each(n_ctr - 1, lambda k: pt_copy(c_me, peer(k)).start())

    ones = jnp.ones((8, feats), BF16)
    cen_copy.wait()

    def scale(k):
        at = pl.ds(pl.multiple_of(k * chunk, chunk), chunk)
        scaled = (cen[at, :].astype(F32) * inv).astype(BF16)
        cen[at, :] = scaled
        square = jnp.square(scaled.astype(F32))
        high = square.astype(BF16)
        low = (square - high.astype(F32)).astype(BF16)
        rnorm[:, at] = 0.5 * (dot_nt(ones, high) + dot_nt(ones, low))
    each(chunks, scale)
    coef_copy.wait()
    pinv_copy.start()
    fac_copy.start()
    head_copy.start()

    each(n_ctr - 1, lambda k: pt_copy(peer(k), peer(k)).wait_recv())

    def group_at(p):
        return pl.ds(pl.multiple_of(p * group, group), group)

    def fw_copy(p_src, p_dst):
        at = group_at(p_src)
        return remote(pall.at[at], pall.at[at], fw_s.at[p_dst], fw_r.at[p_src], p_dst, c_me)

    pair = p_me // 2 * 2

    def mate(k):
        return 2 * pair + 1 - p_me if k == 0 else lax.rem(pair + k + 1, n_pts)
    for k in range(n_pts - 1):
        fw_copy(p_me, mate(k)).start()

    def half_norm(x):
        return 0.5 * jnp.sum(jnp.square(x.astype(F32)), axis=1, keepdims=True)

    def kernel_block(p, k):
        at = pl.ds(pl.multiple_of(k * chunk, chunk), chunk)
        mine = pall[group_at(p), :]
        exponent = dot_nt(mine, cen[at, :]) - half_norm(mine) - rnorm[0:1, at]
        block = jnp.exp(exponent).astype(BF16)
        kmat[group_at(p), at] = block
        return block, at

    def forward(k, total):
        block, at = kernel_block(p_me, k)
        return total + jnp.dot(block, coef[at, :], preferred_element_type=F32)
    total = lax.fori_loop(0, chunks, forward, jnp.zeros((group, targets), F32))
    part[...] = total.reshape(n_ctr, rows, targets)

    def pr_copy(c_src, c_dst):
        return remote(part.at[c_dst], part_recv.at[c_src], pr_s.at[c_dst], pr_r.at[c_src], p_me, c_dst)
    each(n_ctr - 1, lambda k: pr_copy(c_me, peer(k)).start())

    shift, wide_lanes = 64, idx_ref.shape[1]
    per = wide_lanes // n_ctr
    slots = sel.shape[0]
    relative = idx_ref[...] - c_me * centers
    relative = jnp.where((relative >= 0) & (relative < centers), relative, 0)

    def iota(shape, dim):
        return lax.broadcasted_iota(jnp.int32, shape, dim)

    def hot(mask):
        return jnp.where(mask, 1.0, 0.0).astype(BF16)
    fold = hot(iota((wide_lanes, wide_lanes), 0) // n_ctr == iota((wide_lanes, wide_lanes), 1))
    spread = hot(iota((slots, relative.shape[0]), 0) // per == iota((slots, relative.shape[0]), 1))

    def column(value):
        folded = jnp.dot(value.astype(F32).astype(BF16), fold, preferred_element_type=F32)
        return jnp.dot(spread, folded.astype(BF16), preferred_element_type=F32)
    both = shift * column(relative // shift) + column(lax.rem(relative, shift))
    at_lane = lax.rem(iota((slots, wide_lanes), 0), per) == iota((slots, wide_lanes), 1)
    local_row = jnp.sum(jnp.where(at_lane, both, 0.0), axis=1, keepdims=True).astype(jnp.int32)
    sel[...] = jnp.zeros_like(sel)

    def select(k):
        at = pl.ds(pl.multiple_of(k * chunk, chunk), chunk)
        picked = hot(iota((slots, chunk), 1) == local_row - k * chunk)
        sel[...] += jnp.dot(picked, cen[at, :], preferred_element_type=F32)
    each(chunks, select)

    each(n_ctr - 1, lambda k: pr_copy(peer(k), peer(k)).wait_recv())
    part_recv[c_me] = part[c_me]
    predicted = jnp.sum(part_recv[...], axis=0)
    same = iota((rows, rows), 0) == iota((rows, rows), 1)
    own_class = jnp.sum(jnp.where(same, cls_ref[...], 0), axis=1, keepdims=True)
    classes = lax.broadcasted_iota(jnp.int32, (rows, cw_ref.shape[1]), 1)
    weight = jnp.sum(jnp.where(own_class == classes, cw_ref[...], 0.0), axis=1, keepdims=True)
    rall[own_slot, :] = (weight * (predicted - tgt_ref[...])).astype(BF16)

    def rs_copy(src, dst):
        slot = pl.ds(pl.multiple_of(src * rows, rows), rows)
        return remote(
            rall.at[slot], rall.at[slot], rs_s.at[dst], rs_r.at[src], dst // n_ctr, lax.rem(dst, n_ctr)
        )

    def other(k):
        return lax.rem(me + k + 1, everyone)
    each(everyone - 1, lambda k: rs_copy(me, other(k)).start())

    for k in range(n_pts - 1):
        fw_copy(mate(k), mate(k)).wait_recv()
        each(chunks, functools.partial(kernel_block, mate(k)))

    chosen = sel[...].astype(BF16)
    chosen_norm = half_norm(chosen)

    def window_kernel(p):
        mine = pall[group_at(p), :]
        square = jnp.square(mine.astype(F32))
        high = square.astype(BF16)
        low = (square - high.astype(F32)).astype(BF16)
        norm = 0.5 * (dot_nt(ones, high) + dot_nt(ones, low))
        ksel[:, group_at(p)] = jnp.exp(dot_nt(chosen, mine) - norm[0:1] - chosen_norm).astype(BF16)
    each(n_pts, window_kernel)

    each(everyone - 1, lambda k: rs_copy(other(k), other(k)).wait_recv())

    source = lax.broadcasted_iota(jnp.int32, (targets, targets), 0)
    lane = lax.broadcasted_iota(jnp.int32, (targets, targets), 1)
    pick = (source == p_me * tcols + lax.rem(lane, tcols)).astype(BF16)
    wide = jnp.dot(rall[...], pick, preferred_element_type=F32).astype(BF16)
    window = jnp.dot(ksel[...], wide, preferred_element_type=F32)
    run = wsend.shape[1]
    lane_group = lax.broadcasted_iota(jnp.int32, (run, targets), 1) // tcols
    for panel in range(panels):
        packed = jnp.zeros((run, targets), F32)
        for g in range(n_pts):
            begin = (panel * n_pts + g) * run
            packed = packed + jnp.where(lane_group == g, window[begin:begin + run], 0.0)
        wsend[panel] = packed.astype(BF16)

    def w_copy(c_src, c_dst):
        return remote(
            wsend.at[c_dst // owners], wrecv.at[c_src], w_s.at[c_dst], w_r.at[c_src], p_me, c_dst
        )
    each(n_ctr - 1, lambda k: w_copy(c_me, peer(k)).start())
    wrecv[c_me] = wsend[my_panel]

    tall = lax.broadcasted_iota(jnp.int32, (tcols, targets), 1)
    first = lax.broadcasted_iota(jnp.int32, (tcols, targets), 0)
    pick_t = (tall == p_me * tcols + first).astype(BF16)
    wide_t = dot_nt(pick_t, rall[...]).astype(BF16)

    def backward(k):
        at = pl.ds(pl.multiple_of(k * chunk, chunk), chunk)
        grad_ref[:, at] = jnp.dot(wide_t, kmat[:, at], preferred_element_type=F32)
    each(chunks, backward)
    pinv_copy.wait()
    fac_copy.wait()
    head_copy.wait()
    pinv[...] = pinv_raw[...].astype(BF16)

    each(n_ctr - 1, lambda k: w_copy(peer(k), peer(k)).wait_recv())
    for o in range(n_ctr):
        wpack[pl.ds(o, run, stride=n_ctr), :] = wrecv[head[o // wide_lanes, o % wide_lanes] // centers].astype(F32)

    def so_copy(c_src, c_dst):
        return remote(solsend, solrecv.at[c_src], so_s.at[c_dst], so_r.at[c_src], p_me, c_dst)

    def rh_copy(c_src, c_dst):
        at = lax.rem(c_src, owners)
        return remote(rhssend, rhsrecv.at[at], rh_s.at[c_dst], rh_r.at[at], p_me, c_dst)

    for panel in range(panels):
        @pl.when(my_panel == panel)
        def _():
            if panel == 0:
                turned = wpack[...].T.astype(BF16)
                rhs = jnp.concatenate([turned[g * tcols:(g + 1) * tcols] for g in range(n_pts)], axis=1)
            else:
                local = (c_me - panel * owners) * own_rows
                part_len = panel_rows // n_pts
                within = pl.multiple_of(lax.rem(local, part_len), own_rows)
                turned = wpack[pl.ds(within, own_rows), :].T
                for g in range(n_pts):
                    wblk[g] = turned[g * tcols:(g + 1) * tcols]
                own = wblk[local // part_len]
                done = panel * owners
                fac[...] = fac_raw[...].astype(BF16)
                each(done, lambda k: so_copy(k, k).wait_recv())
                solved = jnp.concatenate([solrecv[b] for b in range(done)], axis=1)
                own = own - dot_nt(solved, fac[:, :done * own_rows])
                rhssend[...] = own.astype(BF16)

                def fellow(k):
                    return panel * owners + lax.rem(c_me - panel * owners + k + 1, owners)
                each(owners - 1, lambda k: rh_copy(c_me, fellow(k)).start())
                rhsrecv[c_me - panel * owners] = rhssend[...]
                each(owners - 1, lambda k: rh_copy(fellow(k), fellow(k)).wait_recv())
                rhs = jnp.concatenate([rhsrecv[b] for b in range(owners)], axis=1)
            result = dot_nt(rhs, pinv[...])
            sol_ref[...] = result
            later = (panels - 1 - panel) * owners
            if later:
                solsend[...] = result.astype(BF16)

                def after(k):
                    return (panel + 1) * owners + lax.rem(k + c_me, later)
                each(later, lambda k: so_copy(c_me, after(k)).start())
                each(later, lambda k: so_copy(c_me, after(k)).wait_send())
            if panel > 0:
                each(owners - 1, lambda k: rh_copy(c_me, fellow(k)).wait_send())

    each(n_ctr - 1, lambda k: pt_copy(c_me, peer(k)).wait_send())
    for k in range(n_pts - 1):
        fw_copy(p_me, mate(k)).wait_send()
    each(n_ctr - 1, lambda k: pr_copy(c_me, peer(k)).wait_send())
    each(everyone - 1, lambda k: rs_copy(me, other(k)).wait_send())
    each(n_ctr - 1, lambda k: w_copy(c_me, peer(k)).wait_send())


def body(
    points, point_class, targets, class_weight, inv_scale, centers, coefficients, center_index, factor, panel_inverse
):
    n_pts, n_ctr = lax.axis_size("pts"), lax.axis_size("ctr")
    rows, feats = points.shape
    n_cen, n_tgt = coefficients.shape
    tcols = n_tgt // n_pts
    own_rows, panel_rows = panel_inverse.shape
    panels = factor.shape[1] // panel_rows
    owners = panel_rows // own_rows
    everyone = n_pts * n_ctr
    total = rows * everyone
    slots = center_index.shape[0] // n_ctr
    run = slots // panels // n_pts
    solved_cols = panel_rows * (panels - 1)
    index = center_index.reshape(-1, 128)
    vmem = pl.BlockSpec(memory_space=pltpu.VMEM)
    hbm = pl.BlockSpec(memory_space=pl.ANY)
    dma = pltpu.SemaphoreType.DMA
    scratch = [
        pltpu.VMEM((n_cen, feats), BF16),
        pltpu.VMEM((n_cen, n_tgt), BF16),
        pltpu.VMEM((own_rows, panel_rows), F32),
        pltpu.VMEM((own_rows, panel_rows), BF16),
        pltpu.VMEM((own_rows, solved_cols), F32),
        pltpu.VMEM((own_rows, solved_cols), BF16),
        pltpu.VMEM((8, n_cen), F32),
        pltpu.VMEM((total, feats), BF16),
        pltpu.VMEM((total, n_cen), BF16),
        pltpu.VMEM((slots, total), BF16),
        pltpu.SMEM((8, 128), jnp.int32),
        pltpu.VMEM((slots, feats), F32),
        pltpu.VMEM((n_ctr, rows, n_tgt), F32),
        pltpu.VMEM((n_ctr, rows, n_tgt), F32),
        pltpu.VMEM((total, n_tgt), BF16),
        pltpu.VMEM((panels, run, n_tgt), BF16),
        pltpu.VMEM((n_ctr, run, n_tgt), BF16),
        pltpu.VMEM((run * n_ctr, n_tgt), F32),
        pltpu.VMEM((n_pts, tcols, own_rows), F32),
        pltpu.VMEM((tcols, own_rows), BF16),
        pltpu.VMEM((owners * (panels - 1), tcols, own_rows), BF16),
        pltpu.VMEM((tcols, own_rows), BF16),
        pltpu.VMEM((owners, tcols, own_rows), BF16),
        dma((5,)),
        dma((n_ctr,)), dma((n_ctr,)),
        dma((n_pts,)), dma((n_pts,)),
        dma((n_ctr,)), dma((n_ctr,)),
        dma((everyone,)), dma((everyone,)),
        dma((n_ctr,)), dma((n_ctr,)),
        dma((n_ctr,)), dma((n_ctr,)),
        dma((n_ctr,)), dma((owners,)),
    ]
    grad, solved = pl.pallas_call(
        functools.partial(kernel, n_pts, n_ctr, panels, 512),
        out_shape=(
            jax.ShapeDtypeStruct((tcols, n_cen), F32),
            jax.ShapeDtypeStruct((tcols, own_rows), F32),
        ),
        in_specs=[vmem] * 6 + [hbm] * 5,
        out_specs=(vmem, vmem),
        scratch_shapes=scratch,
        compiler_params=pltpu.CompilerParams(
            collective_id=0, has_side_effects=True, vmem_limit_bytes=67043328
        ),
        name="falkon",
    )(
        points, point_class[None, :], targets, class_weight[None, :], inv_scale[None, :],
        index, index, centers, coefficients, factor, panel_inverse,
    )
    return grad.T, solved.T


def solution(mesh):
    placed = (
        P(("pts", "ctr"), None),
        P(("pts", "ctr")),
        P(("pts", "ctr"), None),
        P(),
        P(),
        P("ctr", None),
        P("ctr", None),
        P(),
        P("ctr", None),
        P("ctr", None),
    )
    return jax.shard_map(
        body,
        mesh=mesh,
        in_specs=placed,
        out_specs=(P("ctr", "pts"), P("ctr", "pts")),
        check_vma=False,
    )
```

```python
import functools

import jax
import jax.numpy as jnp
from jax import lax
from jax.experimental import pallas as pl
from jax.experimental.pallas import tpu as pltpu
from jax.sharding import PartitionSpec as P

MESH = pl.DeviceIdType.MESH
NT = (((1,), (1,)), ((), ()))
F32 = jnp.float32
BF16 = jnp.bfloat16


def dot_nt(left, right):
    return lax.dot_general(left, right, NT, preferred_element_type=F32)


def kernel(
    n_pts, n_ctr, panels, chunk,
    pts_ref, cls_ref, tgt_ref, cw_ref, inv_ref, idx_ref, idx_hbm, cen_hbm, coef_hbm, fac_hbm, pinv_hbm,
    grad_ref, sol_ref,
    cen, coef, pinv_raw, pinv, fac_raw, fac, rnorm, pall, kmat, ksel,
    head, sel, part, part_recv, rall, wsend, wrecv, wpack, wblk, solsend, solrecv, rhssend, rhsrecv,
    loc, pt_s, pt_r, fw_s, fw_r, pr_s, pr_r, rs_s, rs_r, w_s, w_r, so_s, so_r, rh_s, rh_r,
):
    p_me, c_me = lax.axis_index("pts"), lax.axis_index("ctr")
    rows = pts_ref.shape[0]
    group = rows * n_ctr
    centers = cen.shape[0]
    feats = cen.shape[1]
    targets = tgt_ref.shape[1]
    tcols = targets // n_pts
    own_rows = pinv.shape[0]
    panel_rows = pinv.shape[1]
    owners = panel_rows // own_rows
    my_panel = c_me // owners
    chunks = centers // chunk

    def remote(src, dst, send, recv, p, c):
        return pltpu.make_async_remote_copy(
            src_ref=src, dst_ref=dst, send_sem=send, recv_sem=recv,
            device_id={"pts": p, "ctr": c}, device_id_type=MESH,
        )

    def each(n, fn):
        def step(k, carry):
            fn(k)
            return carry
        lax.fori_loop(0, n, step, 0)

    barrier = pltpu.get_barrier_semaphore()
    everyone = n_pts * n_ctr
    me = p_me * n_ctr + c_me

    def greet(k):
        other = lax.rem(me + k + 1, everyone)
        pl.semaphore_signal(
            barrier, inc=1,
            device_id={"pts": other // n_ctr, "ctr": lax.rem(other, n_ctr)}, device_id_type=MESH,
        )
    cen_copy = pltpu.make_async_copy(cen_hbm, cen, loc.at[0])
    coef_copy = pltpu.make_async_copy(coef_hbm, coef, loc.at[1])
    pinv_copy = pltpu.make_async_copy(pinv_hbm, pinv_raw, loc.at[2])
    fac_copy = pltpu.make_async_copy(fac_hbm.at[:, pl.ds(0, fac.shape[1])], fac_raw, loc.at[3])
    head_copy = pltpu.make_async_copy(idx_hbm.at[pl.ds(0, head.shape[0])], head, loc.at[4])
    cen_copy.start()
    each(everyone - 1, greet)
    coef_copy.start()

    inv = inv_ref[...]
    own_slot = pl.ds(pl.multiple_of(me * rows, rows), rows)
    pall[own_slot, :] = (pts_ref[...].astype(F32) * inv).astype(BF16)
    pl.semaphore_wait(barrier, everyone - 1)

    def pt_copy(c_src, c_dst):
        slot = pl.ds(pl.multiple_of((p_me * n_ctr + c_src) * rows, rows), rows)
        return remote(pall.at[slot], pall.at[slot], pt_s.at[c_dst], pt_r.at[c_src], p_me, c_dst)

    def peer(k):
        return lax.rem(c_me + k + 1, n_ctr)
    each(n_ctr - 1, lambda k: pt_copy(c_me, peer(k)).start())

    ones = jnp.ones((8, feats), BF16)
    cen_copy.wait()

    def scale(k):
        at = pl.ds(pl.multiple_of(k * chunk, chunk), chunk)
        scaled = (cen[at, :].astype(F32) * inv).astype(BF16)
        cen[at, :] = scaled
        square = jnp.square(scaled.astype(F32))
        high = square.astype(BF16)
        low = (square - high.astype(F32)).astype(BF16)
        rnorm[:, at] = 0.5 * (dot_nt(ones, high) + dot_nt(ones, low))
    each(chunks, scale)
    coef_copy.wait()
    pinv_copy.start()
    fac_copy.start()
    head_copy.start()

    each(n_ctr - 1, lambda k: pt_copy(peer(k), peer(k)).wait_recv())

    def group_at(p):
        return pl.ds(pl.multiple_of(p * group, group), group)

    def fw_copy(p_src, p_dst):
        at = group_at(p_src)
        return remote(pall.at[at], pall.at[at], fw_s.at[p_dst], fw_r.at[p_src], p_dst, c_me)

    pair = p_me // 2 * 2

    def mate(k):
        return 2 * pair + 1 - p_me if k == 0 else lax.rem(pair + k + 1, n_pts)
    for k in range(n_pts - 1):
        fw_copy(p_me, mate(k)).start()

    def half_norm(x):
        return 0.5 * jnp.sum(jnp.square(x.astype(F32)), axis=1, keepdims=True)

    def kernel_block(p, k):
        at = pl.ds(pl.multiple_of(k * chunk, chunk), chunk)
        mine = pall[group_at(p), :]
        exponent = dot_nt(mine, cen[at, :]) - half_norm(mine) - rnorm[0:1, at]
        block = jnp.exp(exponent).astype(BF16)
        kmat[group_at(p), at] = block
        return block, at

    def forward(k, total):
        block, at = kernel_block(p_me, k)
        return total + jnp.dot(block, coef[at, :], preferred_element_type=F32)
    total = lax.fori_loop(0, chunks, forward, jnp.zeros((group, targets), F32))
    part[...] = total.reshape(n_ctr, rows, targets)

    def pr_copy(c_src, c_dst):
        return remote(part.at[c_dst], part_recv.at[c_src], pr_s.at[c_dst], pr_r.at[c_src], p_me, c_dst)
    each(n_ctr - 1, lambda k: pr_copy(c_me, peer(k)).start())

    shift, wide_lanes = 64, idx_ref.shape[1]
    per = wide_lanes // n_ctr
    slots = sel.shape[0]
    relative = idx_ref[...] - c_me * centers
    relative = jnp.where((relative >= 0) & (relative < centers), relative, 0)

    def iota(shape, dim):
        return lax.broadcasted_iota(jnp.int32, shape, dim)

    def hot(mask):
        return jnp.where(mask, 1.0, 0.0).astype(BF16)
    fold = hot(iota((wide_lanes, wide_lanes), 0) // n_ctr == iota((wide_lanes, wide_lanes), 1))
    spread = hot(iota((slots, relative.shape[0]), 0) // per == iota((slots, relative.shape[0]), 1))

    def column(value):
        folded = jnp.dot(value.astype(F32).astype(BF16), fold, preferred_element_type=F32)
        return jnp.dot(spread, folded.astype(BF16), preferred_element_type=F32)
    both = shift * column(relative // shift) + column(lax.rem(relative, shift))
    at_lane = lax.rem(iota((slots, wide_lanes), 0), per) == iota((slots, wide_lanes), 1)
    local_row = jnp.sum(jnp.where(at_lane, both, 0.0), axis=1, keepdims=True).astype(jnp.int32)
    sel[...] = jnp.zeros_like(sel)

    def select(k):
        at = pl.ds(pl.multiple_of(k * chunk, chunk), chunk)
        picked = hot(iota((slots, chunk), 1) == local_row - k * chunk)
        sel[...] += jnp.dot(picked, cen[at, :], preferred_element_type=F32)
    each(chunks, select)

    each(n_ctr - 1, lambda k: pr_copy(peer(k), peer(k)).wait_recv())
    part_recv[c_me] = part[c_me]
    predicted = jnp.sum(part_recv[...], axis=0)
    same = iota((rows, rows), 0) == iota((rows, rows), 1)
    own_class = jnp.sum(jnp.where(same, cls_ref[...], 0), axis=1, keepdims=True)
    classes = lax.broadcasted_iota(jnp.int32, (rows, cw_ref.shape[1]), 1)
    weight = jnp.sum(jnp.where(own_class == classes, cw_ref[...], 0.0), axis=1, keepdims=True)
    rall[own_slot, :] = (weight * (predicted - tgt_ref[...])).astype(BF16)

    def rs_copy(src, dst):
        slot = pl.ds(pl.multiple_of(src * rows, rows), rows)
        return remote(
            rall.at[slot], rall.at[slot], rs_s.at[dst], rs_r.at[src], dst // n_ctr, lax.rem(dst, n_ctr)
        )

    def other(k):
        return lax.rem(me + k + 1, everyone)
    each(everyone - 1, lambda k: rs_copy(me, other(k)).start())

    for k in range(n_pts - 1):
        fw_copy(mate(k), mate(k)).wait_recv()
        each(chunks, functools.partial(kernel_block, mate(k)))

    chosen = sel[...].astype(BF16)
    chosen_norm = half_norm(chosen)

    def window_kernel(p):
        mine = pall[group_at(p), :]
        square = jnp.square(mine.astype(F32))
        high = square.astype(BF16)
        low = (square - high.astype(F32)).astype(BF16)
        norm = 0.5 * (dot_nt(ones, high) + dot_nt(ones, low))
        ksel[:, group_at(p)] = jnp.exp(dot_nt(chosen, mine) - norm[0:1] - chosen_norm).astype(BF16)
    each(n_pts, window_kernel)

    each(everyone - 1, lambda k: rs_copy(other(k), other(k)).wait_recv())

    source = lax.broadcasted_iota(jnp.int32, (targets, targets), 0)
    lane = lax.broadcasted_iota(jnp.int32, (targets, targets), 1)
    pick = (source == p_me * tcols + lax.rem(lane, tcols)).astype(BF16)
    wide = jnp.dot(rall[...], pick, preferred_element_type=F32).astype(BF16)
    window = jnp.dot(ksel[...], wide, preferred_element_type=F32)
    run = wsend.shape[1]
    lane_group = lax.broadcasted_iota(jnp.int32, (run, targets), 1) // tcols
    for panel in range(panels):
        packed = jnp.zeros((run, targets), F32)
        for g in range(n_pts):
            begin = (panel * n_pts + g) * run
            packed = packed + jnp.where(lane_group == g, window[begin:begin + run], 0.0)
        wsend[panel] = packed.astype(BF16)

    def w_copy(c_src, c_dst):
        return remote(
            wsend.at[c_dst // owners], wrecv.at[c_src], w_s.at[c_dst], w_r.at[c_src], p_me, c_dst
        )
    each(n_ctr - 1, lambda k: w_copy(c_me, peer(k)).start())
    wrecv[c_me] = wsend[my_panel]

    tall = lax.broadcasted_iota(jnp.int32, (tcols, targets), 1)
    first = lax.broadcasted_iota(jnp.int32, (tcols, targets), 0)
    pick_t = (tall == p_me * tcols + first).astype(BF16)
    wide_t = dot_nt(pick_t, rall[...]).astype(BF16)

    def backward(k):
        at = pl.ds(pl.multiple_of(k * chunk, chunk), chunk)
        grad_ref[:, at] = jnp.dot(wide_t, kmat[:, at], preferred_element_type=F32)
    each(chunks, backward)
    pinv_copy.wait()
    fac_copy.wait()
    head_copy.wait()
    pinv[...] = pinv_raw[...].astype(BF16)

    each(n_ctr - 1, lambda k: w_copy(peer(k), peer(k)).wait_recv())
    for o in range(n_ctr):
        wpack[pl.ds(o, run, stride=n_ctr), :] = wrecv[head[o // wide_lanes, o % wide_lanes] // centers].astype(F32)

    def so_copy(c_src, c_dst):
        return remote(solsend, solrecv.at[c_src], so_s.at[c_dst], so_r.at[c_src], p_me, c_dst)

    def rh_copy(c_src, c_dst):
        at = lax.rem(c_src, owners)
        return remote(rhssend, rhsrecv.at[at], rh_s.at[c_dst], rh_r.at[at], p_me, c_dst)

    for panel in range(panels):
        @pl.when(my_panel == panel)
        def _():
            if panel == 0:
                turned = wpack[...].T.astype(BF16)
                rhs = jnp.concatenate([turned[g * tcols:(g + 1) * tcols] for g in range(n_pts)], axis=1)
            else:
                local = (c_me - panel * owners) * own_rows
                part_len = panel_rows // n_pts
                within = pl.multiple_of(lax.rem(local, part_len), own_rows)
                turned = wpack[pl.ds(within, own_rows), :].T
                for g in range(n_pts):
                    wblk[g] = turned[g * tcols:(g + 1) * tcols]
                own = wblk[local // part_len]
                done = panel * owners
                fac[...] = fac_raw[...].astype(BF16)
                each(done, lambda k: so_copy(k, k).wait_recv())
                solved = jnp.concatenate([solrecv[b] for b in range(done)], axis=1)
                own = own - dot_nt(solved, fac[:, :done * own_rows])
                rhssend[...] = own.astype(BF16)

                def fellow(k):
                    return panel * owners + lax.rem(c_me - panel * owners + k + 1, owners)
                each(owners - 1, lambda k: rh_copy(c_me, fellow(k)).start())
                rhsrecv[c_me - panel * owners] = rhssend[...]
                each(owners - 1, lambda k: rh_copy(fellow(k), fellow(k)).wait_recv())
                rhs = jnp.concatenate([rhsrecv[b] for b in range(owners)], axis=1)
            result = dot_nt(rhs, pinv[...])
            sol_ref[...] = result
            later = (panels - 1 - panel) * owners
            if later:
                solsend[...] = result.astype(BF16)

                def after(k):
                    return (panel + 1) * owners + lax.rem(k + c_me, later)
                each(later, lambda k: so_copy(c_me, after(k)).start())
                each(later, lambda k: so_copy(c_me, after(k)).wait_send())
            if panel > 0:
                each(owners - 1, lambda k: rh_copy(c_me, fellow(k)).wait_send())

    each(n_ctr - 1, lambda k: pt_copy(c_me, peer(k)).wait_send())
    for k in range(n_pts - 1):
        fw_copy(p_me, mate(k)).wait_send()
    each(n_ctr - 1, lambda k: pr_copy(c_me, peer(k)).wait_send())
    each(everyone - 1, lambda k: rs_copy(me, other(k)).wait_send())
    each(n_ctr - 1, lambda k: w_copy(c_me, peer(k)).wait_send())


def body(
    points, point_class, targets, class_weight, inv_scale, centers, coefficients, center_index, factor, panel_inverse
):
    n_pts, n_ctr = lax.axis_size("pts"), lax.axis_size("ctr")
    rows, feats = points.shape
    n_cen, n_tgt = coefficients.shape
    tcols = n_tgt // n_pts
    own_rows, panel_rows = panel_inverse.shape
    panels = factor.shape[1] // panel_rows
    owners = panel_rows // own_rows
    everyone = n_pts * n_ctr
    total = rows * everyone
    slots = center_index.shape[0] // n_ctr
    run = slots // panels // n_pts
    solved_cols = panel_rows * (panels - 1)
    index = center_index.reshape(-1, 128)
    vmem = pl.BlockSpec(memory_space=pltpu.VMEM)
    hbm = pl.BlockSpec(memory_space=pl.ANY)
    dma = pltpu.SemaphoreType.DMA
    scratch = [
        pltpu.VMEM((n_cen, feats), BF16),
        pltpu.VMEM((n_cen, n_tgt), BF16),
        pltpu.VMEM((own_rows, panel_rows), F32),
        pltpu.VMEM((own_rows, panel_rows), BF16),
        pltpu.VMEM((own_rows, solved_cols), F32),
        pltpu.VMEM((own_rows, solved_cols), BF16),
        pltpu.VMEM((8, n_cen), F32),
        pltpu.VMEM((total, feats), BF16),
        pltpu.VMEM((total, n_cen), BF16),
        pltpu.VMEM((slots, total), BF16),
        pltpu.SMEM((8, 128), jnp.int32),
        pltpu.VMEM((slots, feats), F32),
        pltpu.VMEM((n_ctr, rows, n_tgt), F32),
        pltpu.VMEM((n_ctr, rows, n_tgt), F32),
        pltpu.VMEM((total, n_tgt), BF16),
        pltpu.VMEM((panels, run, n_tgt), BF16),
        pltpu.VMEM((n_ctr, run, n_tgt), BF16),
        pltpu.VMEM((run * n_ctr, n_tgt), F32),
        pltpu.VMEM((n_pts, tcols, own_rows), F32),
        pltpu.VMEM((tcols, own_rows), BF16),
        pltpu.VMEM((owners * (panels - 1), tcols, own_rows), BF16),
        pltpu.VMEM((tcols, own_rows), BF16),
        pltpu.VMEM((owners, tcols, own_rows), BF16),
        dma((5,)),
        dma((n_ctr,)), dma((n_ctr,)),
        dma((n_pts,)), dma((n_pts,)),
        dma((n_ctr,)), dma((n_ctr,)),
        dma((everyone,)), dma((everyone,)),
        dma((n_ctr,)), dma((n_ctr,)),
        dma((n_ctr,)), dma((n_ctr,)),
        dma((n_ctr,)), dma((owners,)),
    ]
    grad, solved = pl.pallas_call(
        functools.partial(kernel, n_pts, n_ctr, panels, 1024),
        out_shape=(
            jax.ShapeDtypeStruct((tcols, n_cen), F32),
            jax.ShapeDtypeStruct((tcols, own_rows), F32),
        ),
        in_specs=[vmem] * 6 + [hbm] * 5,
        out_specs=(vmem, vmem),
        scratch_shapes=scratch,
        compiler_params=pltpu.CompilerParams(
            collective_id=0, has_side_effects=True, vmem_limit_bytes=67043328
        ),
        name="falkon",
    )(
        points, point_class[None, :], targets, class_weight[None, :], inv_scale[None, :],
        index, index, centers, coefficients, factor, panel_inverse,
    )
    return grad.T, solved.T


def solution(mesh):
    placed = (
        P(("pts", "ctr"), None),
        P(("pts", "ctr")),
        P(("pts", "ctr"), None),
        P(),
        P(),
        P("ctr", None),
        P("ctr", None),
        P(),
        P("ctr", None),
        P("ctr", None),
    )
    return jax.shard_map(
        body,
        mesh=mesh,
        in_specs=placed,
        out_specs=(P("ctr", "pts"), P("ctr", "pts")),
        check_vma=False,
    )
```
